32 devices in a mesh: dp: 16 (over z, x, core), tensor: 2 (over y).
Axes of the slice: x: 2, y: 2, z: 4, core: 2. Of those that a mesh axis runs over, the one named last changes fastest.
Arguments:
- clip_input: bfloat16 [16, 640, 1280], P('dp'), may hold values from -6 to 6
- cotangent: bfloat16 [16, 640, 1280], P('dp'), may hold values from -18 to 18
- lengths: int32 [16], P('dp'), may hold values from 320 to 640, as said below
- attn_gain: float32 [1280], replicated, may hold values from 0.5 to 1.5
- attn_shift: float32 [1280], replicated, may hold values from -3 to 3
- in_weights: bfloat16 [3, 1280, 1280], P(None, None, 'tensor'), may hold values from -0.15625 to 0.15625
- query_bias: float32 [1280], P('tensor'), may hold values from -3 to 3
- value_bias: float32 [1280], P('tensor'), may hold values from -0.3 to 0.3
- out_weights: bfloat16 [1280, 1280], P('tensor'), may hold values from -2.5 to 2.5
- out_bias: float32 [1280], replicated, may hold values from -2 to 2
- mlp_gain: float32 [1280], replicated, may hold values from 0.5 to 1.5
- mlp_shift: float32 [1280], replicated, may hold values from -3 to 3
- up_weights: bfloat16 [1280, 5120], P(None, 'tensor'), may hold values from -0.15625 to 0.15625
- up_bias: float32 [5120], P('tensor'), may hold values from -3 to 3
- down_weights: bfloat16 [5120, 1280], P('tensor'), may hold values from -0.15625 to 0.15625
- down_bias: float32 [1280], replicated, may hold values from -2 to 2
Outputs:
- activations: bfloat16 [16, 640, 1280], P('dp', 'tensor')
- input_grad: float32 [16, 640, 1280], P('dp', 'tensor')
- attn_gain_grad: float32 [1280], replicated
- attn_shift_grad: float32 [1280], replicated
- in_weights_grad: float32 [3, 1280, 1280], P(None, None, 'tensor')
- query_bias_grad: float32 [1280], P('tensor')
- value_bias_grad: float32 [1280], P('tensor')
- out_weights_grad: float32 [1280, 1280], P('tensor')
- out_bias_grad: float32 [1280], replicated
- mlp_gain_grad: float32 [1280], replicated
- mlp_shift_grad: float32 [1280], replicated
- up_weights_grad: float32 [1280, 5120], P(None, 'tensor')
- up_bias_grad: float32 [5120], P('tensor')
- down_weights_grad: float32 [5120, 1280], P('tensor')
- down_bias_grad: float32 [1280], replicated
The draws below stay inside these ranges and needn't reach their ends.
Inputs may be any that keep to these rules, and one draw needn't show every extreme that they name: Clip c holds lengths[c] valid tokens at its first positions; keys at later positions are masked. Some clip is full in every draw.
All inputs are finite; a program needn't handle non-finite values.
Results may differ from the reference program's by a relative error of at most 0.02.
Values may be sent and summed in bfloat16 or wider, within the bound.
No kernel may reach another device: no remote copies, remote signals or barrier semaphores. Data moves between devices by JAX's collectives and lax.ppermute only.
A program may use at most 256 MiB of HBM per device.

```python
import math
import jax
import jax.numpy as jnp
from jax import lax

D = 1280
H = 16
HD = 80
FF = 5120
LEN = 640
QBLK = 640
CLIPS = 16
N_TENSOR = 2


def draw_cotangent(key, part):
    rise = jnp.exp(math.log(3.0) * jnp.arange(CLIPS, dtype=jnp.float32) / max(CLIPS - 1, 1))
    values = jnp.clip(jax.random.normal(key, (CLIPS, LEN, D), jnp.float32), -6.0, 6.0)
    return (values * rise[:, None, None]).astype(jnp.bfloat16)


def draw_lengths(key, part):
    counts = jax.random.randint(key, (CLIPS,), LEN // 2, LEN + 1)
    where = jax.random.randint(jax.random.fold_in(key, 11), (), 0, CLIPS)
    return counts.at[where].set(LEN).astype(jnp.int32)


def shard_levels(rng, shape, cuts, least, high):
    factor_of, own = 1.0, jax.random.fold_in(rng, 6)
    for axis_at, shards_of in cuts:
        draws = jnp.exp(jax.random.uniform(jax.random.fold_in(own, axis_at), (shards_of,), jnp.float32, least / len(cuts), high / len(cuts)))
        factor_of = factor_of * jnp.repeat(draws, shape[axis_at] // shards_of).reshape([-1 if axis == axis_at else 1 for axis in range(len(shape))])
    return factor_of


def noise(key, extent, scale, limit, pieces=(), held_as=jnp.bfloat16):
    level = shard_levels(key, extent, pieces, -0.22, 0.18) if pieces else 1.0
    entries = jax.random.normal(key, extent, jnp.float32) * scale * level
    return jnp.minimum(jnp.maximum(entries, -limit), limit).astype(held_as)


def setup_inputs(seed: int = 0) -> dict:
    arg_keys = jax.random.split(jax.random.key(seed), 17)
    return {
        "clip_input": noise(arg_keys[0], (CLIPS, LEN, D), 1.0, 6.0, ((0, 16),)),
        "cotangent": draw_cotangent(jax.random.fold_in(arg_keys[16], 71), 0),
        "lengths": draw_lengths(jax.random.fold_in(arg_keys[16], 71), 0),
        "attn_gain": jnp.clip(1.0 + 0.1 * jax.random.normal(arg_keys[3], (D,), jnp.float32), 0.5, 1.5),
        "attn_shift": noise(arg_keys[4], (D,), 0.5, 3.0, (), jnp.float32),
        "in_weights": noise(arg_keys[5], (3, D, H * HD), D ** -0.5, 0.15625, ((2, 2),)),
        "query_bias": noise(arg_keys[6], (H * HD,), 0.5, 3.0, ((0, 2),), jnp.float32),
        "value_bias": noise(arg_keys[7], (H * HD,), 0.05, 0.3, ((0, 2),), jnp.float32),
        "out_weights": noise(arg_keys[8], (H * HD, D), (max(H * HD // 256, 1)) ** -0.5, 2.5, ((0, 2),)),
        "out_bias": noise(arg_keys[9], (D,), 0.3, 2.0, (), jnp.float32),
        "mlp_gain": jnp.clip(1.0 + 0.1 * jax.random.normal(arg_keys[10], (D,), jnp.float32), 0.5, 1.5),
        "mlp_shift": noise(arg_keys[11], (D,), 0.5, 3.0, (), jnp.float32),
        "up_weights": noise(arg_keys[12], (D, FF), D ** -0.5, 0.15625, ((1, 2),)),
        "up_bias": noise(arg_keys[13], (FF,), 0.5, 3.0, ((0, 2),), jnp.float32),
        "down_weights": noise(arg_keys[14], (FF, D), (FF // 4) ** -0.5, 0.15625, ((0, 2),)),
        "down_bias": noise(arg_keys[15], (D,), 0.3, 2.0, (), jnp.float32),
    }


@jax.custom_vjp
def low(v):
    return lax.optimization_barrier(v.astype(jnp.bfloat16)).astype(jnp.float32)

@jax.custom_vjp
def low_back(v):
    return v

def low_keep(v):
    return (low(v), None)

def low_pass(kept, grad):
    return (grad,)

def back_keep(v):
    return (v, None)

def back_low(kept, grad):
    return (low(grad),)
low.defvjp(low_keep, low_pass)
low_back.defvjp(back_keep, back_low)
EPS = 1e-05
NEG = -1e+30
HIGH = lax.Precision.HIGHEST

def norm_rows(rows, gain, shift):
    centred = rows - lax.optimization_barrier(jnp.mean(rows, axis=-1, keepdims=True))
    rstd = lax.rsqrt(lax.optimization_barrier(jnp.mean(centred * centred, axis=-1, keepdims=True)) + EPS)
    return centred * rstd * gain + shift

def attend_block(qblock, keys, values, valid):
    scores = jnp.einsum('bhe,khe->hbk', qblock, keys, precision=HIGH) * (1.0 / math.sqrt(HD))
    scores = jnp.where(valid[None, None, :], scores, NEG)
    scores = low_back(scores)
    top = lax.optimization_barrier(jnp.max(scores, axis=-1, keepdims=True))
    expo = jnp.exp(scores - top)
    probs = expo / lax.optimization_barrier(jnp.sum(expo, axis=-1, keepdims=True))
    probs = low(probs)
    return jnp.einsum('hbk,khe->bhe', probs, values, precision=HIGH)

def clip_forward(params, clip_rows, length):
    attn_gain, attn_shift, in_weights, query_bias, value_bias, out_weights, out_bias, mlp_gain, mlp_shift, up_weights, up_bias, down_weights, down_bias = params
    first = low(norm_rows(clip_rows, attn_gain, attn_shift))
    query = low(low_back(jnp.dot(first, in_weights[0], precision=HIGH)) + query_bias)
    keys = low(low_back(jnp.dot(first, in_weights[1], precision=HIGH)))
    values = low(low_back(jnp.dot(first, in_weights[2], precision=HIGH)) + value_bias)
    query = query.reshape(LEN, H, HD)
    keys = keys.reshape(LEN, H, HD)
    values = values.reshape(LEN, H, HD)
    valid = jnp.arange(LEN) < length
    blocks = query.reshape(LEN // QBLK, QBLK, H, HD)
    block_fn = jax.checkpoint(lambda qblock: attend_block(qblock, keys, values, valid))
    attended = lax.map(block_fn, blocks).reshape(LEN, H * HD)
    attended = low(low_back(attended))
    groups = attended.reshape(LEN, N_TENSOR, H * HD // N_TENSOR)
    wgroups = out_weights.reshape(N_TENSOR, H * HD // N_TENSOR, D)
    partial_terms = low(jnp.einsum('rgc,gcd->grd', groups, wgroups, precision=HIGH))
    mixed = clip_rows + low_back(lax.optimization_barrier(jnp.sum(partial_terms, axis=0))) + out_bias
    second = low(norm_rows(mixed, mlp_gain, mlp_shift))
    pre = low_back(jnp.dot(second, up_weights, precision=HIGH)) + up_bias
    act = low(jax.nn.gelu(pre, approximate=False))
    return mixed + jnp.dot(act, down_weights, precision=HIGH) + down_bias

def reference(clip_input, cotangent, lengths, attn_gain, attn_shift, in_weights, query_bias, value_bias, out_weights, out_bias, mlp_gain, mlp_shift, up_weights, up_bias, down_weights, down_bias):
    params = tuple((p.astype(jnp.float32) for p in (attn_gain, attn_shift, in_weights, query_bias, value_bias, out_weights, out_bias, mlp_gain, mlp_shift, up_weights, up_bias, down_weights, down_bias)))

    def layer(inputs, *weights):
        clip_fn = jax.checkpoint(lambda item: clip_forward(weights, item[0], item[1]))
        return lax.map(clip_fn, (inputs, lengths.astype(jnp.int32)))
    result, pullback = jax.vjp(layer, clip_input.astype(jnp.float32), *params)
    grads = pullback(cotangent.astype(jnp.float32))
    return (result.astype(jnp.bfloat16), grads[0], grads[1], grads[2], grads[3], grads[4], grads[5], grads[6], grads[7], grads[8], grads[9], grads[10], grads[11], grads[12], grads[13])
```

```python
import math

import jax
import jax.numpy as jnp
from jax import lax
from jax.sharding import PartitionSpec as P

HD = 80
QBLK = 640


def position(z, x, core):
    return (z * 2 + x) * 2 + core


CHIPS = [(z, x, core) for z in range(4) for x in range(2) for core in range(2)]
TO_CORE = [(position(z, x, c), position(z, x, 1 - c)) for z, x, c in CHIPS]
TO_X = [(position(z, x, c), position(z, 1 - x, c)) for z, x, c in CHIPS]
TO_X_INNER = [(position(z, x, c), position(z, 1 - x, c)) for z, x, c in CHIPS if z in (1, 2)]
INWARD = [(position(z, x, c), position(1 if z == 0 else 2, x, c)) for z, x, c in CHIPS if z in (0, 3)]
OUTWARD = [(b, a) for a, b in INWARD]
MIDDLE = [(position(z, x, c), position(3 - z, x, c)) for z, x, c in CHIPS if z in (1, 2)]
TO_Y = [(0, 1), (1, 0)]
CYCLE = [(0, 0), (1, 0), (2, 0), (3, 0), (3, 1), (2, 1), (1, 1), (0, 1)]
NEXT = CYCLE[1:] + CYCLE[:1]
RING = [(position(*a, 0), position(*b, 0)) for a, b in zip(CYCLE, NEXT)] + [
    (position(*b, 1), position(*a, 1)) for a, b in zip(CYCLE, NEXT)
]
RANK = [0] * 16
for place_in_cycle, chip in enumerate(CYCLE):
    RANK[position(*chip, 0)] = place_in_cycle
    RANK[position(*chip, 1)] = -place_in_cycle % 8


def add_low(a, b):
    return (a.astype(jnp.float32) + b.astype(jnp.float32)).astype(jnp.bfloat16)


def rows_of(array, start, count):
    return lax.dynamic_slice_in_dim(array, start, count, 0)


def move(array, pairs):
    return lax.ppermute(array, "dp", pairs)


def swap_y(array):
    return lax.ppermute(array, "tensor", TO_Y)


def place(mine, other, which):
    first = which == 0
    return jnp.concatenate([jnp.where(first, mine, other), jnp.where(first, other, mine)], 0)


class Order:
    def __init__(self):
        self.last = None

    def sent(self, *arrays):
        if self.last is not None:
            arrays = lax.optimization_barrier((*arrays, *self.last))[: len(arrays)]
        self.last = arrays
        return arrays

    def then(self, *arrays):
        if self.last is None:
            return arrays if len(arrays) > 1 else arrays[0]
        out = lax.optimization_barrier((*arrays, *self.last))[: len(arrays)]
        return out if len(arrays) > 1 else out[0]


class Piece:
    HOPS = 2 * len(CYCLE)

    def __init__(self, order, columns):
        self.order, self.columns = order, columns
        at = lax.axis_index("dp")
        self.core = at % 2
        self.rank = jnp.asarray(RANK)[at]
        self.half = columns[0].shape[0] // 2
        self.count = self.half // 8
        self.step = 0

    def block(self, start, count):
        return jnp.concatenate([rows_of(c, start, count) for c in self.columns], 1)

    def mine(self, chunk):
        start = (chunk % 8) * self.count
        return add_low(
            self.block(self.core * self.half + start, self.count), rows_of(self.got, start, self.count)
        )

    def put(self, chunk, rows):
        self.own = lax.dynamic_update_slice_in_dim(self.own, rows, (chunk % 8) * self.count, 0)

    def hop(self):
        step, self.step = self.step, self.step + 1
        if step == 0:
            (send,) = self.order.sent(self.block((1 - self.core) * self.half, self.half))
            self.got = move(send, TO_CORE)
        elif step <= 7:
            part = self.mine(self.rank + 8 - step)
            if step > 1:
                part = add_low(part, self.moving)
            (part,) = self.order.sent(part)
            self.moving = move(part, RING)
        elif step <= 14:
            if step == 8:
                part = add_low(self.mine(self.rank), self.moving)
                self.own = jnp.zeros((self.half, part.shape[1]), part.dtype)
                self.put(self.rank, part)
            else:
                part = self.moving
                self.put(self.rank + 16 - step, part)
            (part,) = self.order.sent(part)
            self.moving = move(part, RING)
        elif step == 15:
            self.put(self.rank + 1, self.moving)
            (self.own,) = self.order.sent(self.own)
            self.got = move(self.own, TO_CORE)

    def result(self):
        return place(self.own, self.got, self.core)


def sum_small(order, rows):
    at = lax.axis_index("dp")
    z = at // 4
    for pairs in (TO_CORE, TO_X, INWARD, MIDDLE):
        rows = rows + move(rows, pairs)
    return jnp.where((z == 0) | (z == 3), move(rows, OUTWARD), rows)


EPS = 1e-05
NEG = -1e30


def layer_norm(rows, gain, shift):
    centred = rows - jnp.mean(rows, axis=-1, keepdims=True)
    rstd = lax.rsqrt(jnp.mean(centred * centred, axis=-1, keepdims=True) + EPS)
    normed = centred * rstd
    return (normed * gain + shift, normed, rstd)


def norm_back(grad, normed, rstd, gain):
    scaled = grad * gain
    inner = scaled - jnp.mean(scaled, axis=-1, keepdims=True)
    inner = inner - normed * jnp.mean(scaled * normed, axis=-1, keepdims=True)
    return rstd * inner


def attend_clip(query, keys, values, length):
    seq, heads, width = query.shape
    scale = 1.0 / math.sqrt(width)
    valid = jnp.arange(seq) < length
    scores = jnp.einsum("bhe,khe->hbk", query, keys, preferred_element_type=jnp.float32) * scale
    scores = jnp.where(valid[None, None, :], scores, NEG)
    top = jnp.max(scores, axis=-1, keepdims=True)
    expo = jnp.exp(scores - top)
    total = jnp.sum(expo, axis=-1, keepdims=True)
    probs = (expo / total).astype(jnp.bfloat16)
    out = jnp.einsum("hbk,khe->bhe", probs, values, preferred_element_type=jnp.float32)
    return (out.astype(jnp.bfloat16), (top + jnp.log(total))[..., 0])


def per_device(
    clip_input,
    cotangent,
    lengths,
    attn_gain,
    attn_shift,
    in_weights,
    query_bias,
    value_bias,
    out_weights,
    out_bias,
    mlp_gain,
    mlp_shift,
    up_weights,
    up_bias,
    down_weights,
    down_bias,
):
    clips, seq, width = clip_input.shape
    members = lax.axis_size("tensor")
    share = seq // members
    start = lax.axis_index("tensor") * share
    total_rows = clips * seq
    heads_here = in_weights.shape[2] // HD

    def own_rows(array):
        return lax.dynamic_slice_in_dim(array.reshape(clips, seq, width), start, share, 1)

    inputs = clip_input.astype(jnp.float32).reshape(total_rows, width)
    first_out, first_hat, first_rstd = layer_norm(inputs, attn_gain, attn_shift)
    first = first_out.astype(jnp.bfloat16)
    projected = jnp.einsum("rd,sde->sre", first, in_weights, preferred_element_type=jnp.float32)
    query = (projected[0] + query_bias).astype(jnp.bfloat16)
    keys = projected[1].astype(jnp.bfloat16)
    values = (projected[2] + value_bias).astype(jnp.bfloat16)
    shape_four = (clips, seq, heads_here, HD)
    query4 = query.reshape(shape_four)
    keys4 = keys.reshape(shape_four)
    values4 = values.reshape(shape_four)


    own_sums = members == 2 and lax.axis_size("dp") == 16
    order = Order()

    def summed_rows(partial):
        if members == 2:
            (partial,) = order.sent(partial)
            return partial.astype(jnp.float32) + swap_y(partial).astype(jnp.float32)
        return lax.psum(partial, "tensor").astype(jnp.float32)

    def summed_own(partial):
        partial = partial.reshape(clips, seq, width)
        if members == 2:
            at = lax.axis_index("tensor")
            mine = lax.dynamic_slice_in_dim(partial, at * share, share, 1)
            other = lax.dynamic_slice_in_dim(partial, (1 - at) * share, share, 1)
            (other,) = order.sent(other)
            return mine.astype(jnp.float32) + swap_y(other).astype(jnp.float32)
        return lax.psum_scatter(partial, "tensor", scatter_dimension=1, tiled=True).astype(
            jnp.float32
        )

    attended, lse = jax.vmap(attend_clip)(query4, keys4, values4, lengths)
    attended = attended.reshape(total_rows, heads_here * HD)
    partial_out = jnp.dot(attended, out_weights, preferred_element_type=jnp.float32).astype(
        jnp.bfloat16
    )
    mixed = inputs + summed_rows(partial_out) + out_bias
    second_out, second_hat, second_rstd = layer_norm(mixed, mlp_gain, mlp_shift)
    second = second_out.astype(jnp.bfloat16)
    mixed_own = own_rows(mixed)
    pre = jnp.dot(second, up_weights, preferred_element_type=jnp.float32) + up_bias

    def gelu_exact(values_in):
        return jax.nn.gelu(values_in, approximate=False)

    act_full, gelu_back = jax.vjp(gelu_exact, pre)
    act = act_full.astype(jnp.bfloat16)
    upstream = cotangent.reshape(total_rows, width)
    upstream_own = own_rows(cotangent.astype(jnp.float32))
    down_grad = jnp.einsum("rf,rd->fd", act, upstream, preferred_element_type=jnp.float32).astype(
        jnp.bfloat16
    )
    down_piece = Piece(order, [down_grad])

    def hop(*pieces):
        if own_sums:
            for piece in pieces:
                piece.hop()

    hop(down_piece)
    d_act = jnp.einsum(
        "rd,fd->rf", order.then(upstream), down_weights, preferred_element_type=jnp.float32
    )
    d_pre = gelu_back(d_act)[0]
    up_bias_sum = jnp.sum(d_pre, axis=0)
    d_pre_low = d_pre.astype(jnp.bfloat16)
    hop(down_piece)
    d_second_part = jnp.einsum(
        "rf,df->rd", order.then(d_pre_low), up_weights, preferred_element_type=jnp.float32
    )
    d_second = summed_rows(d_second_part.astype(jnp.bfloat16))
    up_grad = jnp.einsum(
        "rd,rf->df", order.then(second), d_pre_low, preferred_element_type=jnp.float32
    ).astype(jnp.bfloat16)
    up_piece = Piece(order, [up_grad])
    hop(up_piece)
    partial_mlp = jnp.dot(order.then(act), down_weights, preferred_element_type=jnp.float32)
    hop(down_piece, up_piece)
    mlp_own = summed_own(partial_mlp.astype(jnp.bfloat16))
    d_mixed = upstream.astype(jnp.float32) + norm_back(d_second, second_hat, second_rstd, mlp_gain)
    d_second_own = own_rows(d_second)
    second_hat_own = own_rows(second_hat)
    d_mixed_own = own_rows(d_mixed)
    d_branch = d_mixed.astype(jnp.bfloat16)
    mlp_gain_part = jnp.sum(d_second_own * second_hat_own, axis=(0, 1))
    mlp_shift_part = jnp.sum(d_second_own, axis=(0, 1))
    out_bias_part = jnp.sum(d_mixed_own, axis=(0, 1))
    down_bias_part = jnp.sum(upstream_own, axis=(0, 1))
    d_attended = jnp.einsum(
        "rd,cd->rc", d_branch, out_weights, preferred_element_type=jnp.float32
    ).astype(jnp.bfloat16)
    scale = 1.0 / math.sqrt(HD)
    d_att4 = order.then(d_attended.reshape(shape_four))
    valid = jnp.arange(seq)[None, :] < lengths[:, None]
    scores = jnp.einsum("nbhe,nkhe->nhbk", query4, keys4, preferred_element_type=jnp.float32)
    scores = jnp.where(valid[:, None, None, :], scores * scale, NEG)
    probs = jnp.exp(scores - lse[..., None])
    d_probs = jnp.einsum("nbhe,nkhe->nhbk", d_att4, values4, preferred_element_type=jnp.float32)
    delta = jnp.sum(probs * d_probs, axis=-1, keepdims=True)
    d_scores = (probs * (d_probs - delta)).astype(jnp.bfloat16)
    probs_low = probs.astype(jnp.bfloat16)
    hop(down_piece, up_piece)
    d_values = jnp.einsum(
        "nhbk,nbhe->nkhe", order.then(probs_low), d_att4, preferred_element_type=jnp.float32
    ).reshape(total_rows, heads_here * HD)
    value_grad = jnp.einsum(
        "rd,re->de", first, d_values.astype(jnp.bfloat16), preferred_element_type=jnp.float32
    ).astype(jnp.bfloat16)
    wide = heads_here * HD
    out_grad = jnp.concatenate(
        [
            jnp.einsum("rc,rd->cd", attended, d_branch[:, i * wide : (i + 1) * wide], preferred_element_type=jnp.float32)
            for i in range(width // wide)
        ],
        0,
    ).astype(jnp.bfloat16)
    late_piece = Piece(order, [value_grad, out_grad]) if own_sums else None
    hop(late_piece)
    d_query = (
        jnp.einsum("nhbk,nkhe->nbhe", order.then(d_scores), keys4, preferred_element_type=jnp.float32) * scale
    ).reshape(total_rows, heads_here * HD)
    d_keys = (
        jnp.einsum("nhbk,nbhe->nkhe", d_scores, query4, preferred_element_type=jnp.float32) * scale
    ).reshape(total_rows, heads_here * HD)
    query_bias_sum = jnp.sum(d_query, axis=0)
    value_bias_sum = jnp.sum(d_values, axis=0)
    hop(down_piece, up_piece)
    two = jnp.concatenate([d_query, d_keys], 1).astype(jnp.bfloat16)
    two_grad = jnp.einsum(
        "rd,re->de", order.then(first), two, preferred_element_type=jnp.float32
    ).astype(jnp.bfloat16)
    last_piece = Piece(order, [two_grad]) if own_sums else None
    hop(last_piece, late_piece, down_piece)
    stacked = jnp.stack([d_query, d_keys, d_values]).astype(jnp.bfloat16)
    d_first = jnp.einsum("sre,sde->rd", order.then(stacked), in_weights, preferred_element_type=jnp.float32)
    d_first_own = summed_own(d_first.astype(jnp.bfloat16))
    hop(last_piece, late_piece, up_piece)
    result = (order.then(mixed_own) + mlp_own + down_bias).astype(jnp.bfloat16)
    first_hat_own = own_rows(first_hat)
    first_rstd_own = lax.dynamic_slice_in_dim(first_rstd.reshape(clips, seq, 1), start, share, 1)
    hop(down_piece, last_piece, late_piece, up_piece)
    d_input_own = order.then(d_mixed_own) + norm_back(d_first_own, first_hat_own, first_rstd_own, attn_gain)
    attn_gain_part = jnp.sum(d_first_own * first_hat_own, axis=(0, 1))
    attn_shift_part = jnp.sum(d_first_own, axis=(0, 1))
    replicated = jnp.stack(
        [
            attn_gain_part,
            attn_shift_part,
            out_bias_part,
            mlp_gain_part,
            mlp_shift_part,
            down_bias_part,
        ]
    )
    sharded = jnp.concatenate([query_bias_sum, value_bias_sum, up_bias_sum])
    if own_sums:
        replicated = replicated + swap_y(replicated)
        both = sum_small(order, jnp.concatenate([replicated.reshape(-1), sharded]).reshape(9, 1280))
        both = both.reshape(-1)
        small, biases = both[: 6 * width].reshape(6, width), both[6 * width :]
        pieces = (last_piece, late_piece, down_piece, up_piece)
        while any(piece.step < piece.HOPS for piece in pieces):
            hop(*(piece for piece in pieces if piece.step < piece.HOPS))
        down_sum = down_piece.result().astype(jnp.float32)
        up_sum = order.then(up_piece.result()).astype(jnp.float32)
        last, late = last_piece.result(), late_piece.result()
        in_sum = jnp.stack([last[:, :wide], last[:, wide:], late[:, :wide]]).astype(jnp.float32)
        out_sum = jnp.concatenate([late[:wide, wide:], late[wide:, wide:]], 1).astype(jnp.float32)
    else:
        small = lax.psum(replicated, ("dp", "tensor"))
        biases = lax.psum(sharded, "dp")
        out_grad = jnp.concatenate([out_grad[i * wide : (i + 1) * wide] for i in range(width // wide)], 1)
        in_grad = jnp.stack([two_grad[:, :wide], two_grad[:, wide:], value_grad])
        in_sum, out_sum, up_sum, down_sum = (
            lax.psum(grad, "dp").astype(jnp.float32)
            for grad in (in_grad, out_grad, up_grad, down_grad)
        )
    here = heads_here * HD
    qbias_sum, vbias_sum, upbias_sum = biases[:here], biases[here : 2 * here], biases[2 * here :]
    return (
        result,
        d_input_own,
        small[0],
        small[1],
        in_sum,
        qbias_sum,
        vbias_sum,
        out_sum,
        small[2],
        small[3],
        small[4],
        up_sum,
        upbias_sum,
        down_sum,
        small[5],
    )


def solution(mesh):
    placed = (
        P("dp", None, None),
        P("dp", None, None),
        P("dp"),
        P(),
        P(),
        P(None, None, "tensor"),
        P("tensor"),
        P("tensor"),
        P("tensor", None),
        P(),
        P(),
        P(),
        P(None, "tensor"),
        P("tensor"),
        P("tensor", None),
        P(),
    )
    return jax.shard_map(
        per_device,
        mesh=mesh,
        in_specs=placed,
        out_specs=(
            P("dp", "tensor", None),
            P("dp", "tensor", None),
            P(),
            P(),
            P(None, None, "tensor"),
            P("tensor"),
            P("tensor"),
            P("tensor", None),
            P(),
            P(),
            P(),
            P(None, "tensor"),
            P("tensor"),
            P("tensor", None),
            P(),
        ),
        check_vma=False,
    )
```
